32 devices in a mesh: dp: 4 (over z), context: 2 (over core), tensor: 4 (over y, x).
Axes of the slice: x: 2, y: 2, z: 4, core: 2. Of those that a mesh axis runs over, the one named last changes fastest.
Arguments:
- tokens: bfloat16 [8, 1024, 768], P('dp', 'context'), may hold values from -6 to 6
- segments: int32 [8, 1024], P('dp'), may hold values from 0 to 7, never falling along the last dimension, each value on 1 to 512 neighbouring positions
- cotangent: bfloat16 [8, 1024, 768], P('dp', 'context'), may hold values from -6 to 6
- norm_gain: bfloat16 [768], replicated, may hold values from 0.5 to 1.5
- w_zx: bfloat16 [768, 2, 1536], P('dp', None, 'tensor'), may hold values from -0.21875 to 0.21875
- w_bc: bfloat16 [768, 256], P('dp'), may hold values from -0.21875 to 0.21875
- w_dt: bfloat16 [768, 24], P('dp', 'tensor'), may hold values from -0.21875 to 0.21875
- conv_x: float32 [4, 1536], P(None, 'tensor'), may hold values from -3 to 3
- conv_x_bias: float32 [1536], P('tensor'), may hold values from -1.5 to 1.5
- conv_bc: float32 [4, 256], replicated, may hold values from -3 to 3
- conv_bc_bias: float32 [256], replicated, may hold values from -1.5 to 1.5
- a_log: float32 [24], P('tensor'), may hold values from -2 to 2.5
- dt_bias: float32 [24], P('tensor'), may hold values from -5 to -3
- d_skip: float32 [24], P('tensor'), may hold values from 0.5 to 1.5
- gate_gain: float32 [1536], P('tensor'), may hold values from 0.5 to 1.5
- w_out_t: bfloat16 [768, 1536], P('dp', 'tensor'), may hold values from -0.15625 to 0.15625
Outputs:
- out: bfloat16 [8, 1024, 768], P('dp', 'context')
- grad_tokens: bfloat16 [8, 1024, 768], P('dp', 'context')
- grad_norm_gain: float32 [768], replicated
- grad_w_zx: float32 [768, 2, 1536], P(('dp', 'context'), None, 'tensor')
- grad_w_bc: float32 [768, 256], P(('dp', 'context'))
- grad_w_dt: float32 [768, 24], P(('dp', 'context'), 'tensor')
- grad_conv_x: float32 [4, 1536], P(None, 'tensor')
- grad_conv_x_bias: float32 [1536], P('tensor')
- grad_conv_bc: float32 [4, 256], replicated
- grad_conv_bc_bias: float32 [256], replicated
- grad_a_log: float32 [24], P('tensor')
- grad_dt_bias: float32 [24], P('tensor')
- grad_d_skip: float32 [24], P('tensor')
- grad_gate_gain: float32 [1536], P('tensor')
- grad_w_out_t: float32 [768, 1536], P(('dp', 'context'), 'tensor')
The draws below stay inside these ranges and needn't reach their ends.
Inputs may be any that keep to these rules, and one draw needn't show every extreme that they name: `segments`: along each sequence the ids never fall; a document is a run of tokens with one id.
All inputs are finite; a program needn't handle non-finite values.
Results may differ from the reference program's by a relative error of at most 0.012.
Values may be sent and summed in bfloat16 or wider, within the bound.
A program may use at most 128 MiB of HBM per device.

```python
import math
import jax
import jax.numpy as jnp
import numpy as np
from jax import lax

D = 768
HEADS = 24
HEAD = 64
STATE = 128
CONV = 4
GROUP = 256
LEN = 1024
INNER = 1536
SEQS = 8


def block_scale(key, extent, split, smallest, largest):
    gain = 1.0
    for position, parts in split:
        heights = jax.random.uniform(jax.random.fold_in(jax.random.fold_in(key, 6), position), (parts,), jnp.float32, smallest / len(split), largest / len(split))
        gain = gain * jnp.repeat(jnp.exp(heights), extent[position] // parts).reshape((-1,) + (1,) * (len(extent) - 1 - position))
    return gain


def split_up(amount, total, most, slope):
    loads = [(1 << 20) // math.isqrt(rank ** slope) + 1 for rank in range(2, amount + 1)]
    surplus, holding = total - most - (amount - 1), [1] * (amount - 1)
    while surplus > 0:
        movable = [i for i in range(amount - 1) if holding[i] < most]
        whole, remaining = sum([loads[i] for i in movable]), surplus
        for i in movable:
            addition = min(most - holding[i], max(1, remaining * loads[i] // whole), surplus)
            holding[i] = holding[i] + addition
            surplus = surplus - addition
    return np.array([most] + holding)


def uneven_parts(rng, count, total, most, slope):
    if count == 2:
        one = jax.random.randint(rng, (), max(1, total - most), min(most, total - 1) + 1)
        return jnp.stack([one, total - one])
    tallies = jnp.asarray(split_up(count, total, most, slope), jnp.int32)
    couples = (count - 1) // 2
    giver, receiver = tallies[1:1 + 2 * couples:2], tallies[2:2 + 2 * couples:2]
    room = jnp.minimum(giver - 1, most - receiver)
    passed = jax.random.randint(jax.random.fold_in(rng, 1), (couples,), 0, 1 << 20) % (room + 1)
    tallies = tallies.at[1:1 + 2 * couples:2].set(giver - passed).at[2:2 + 2 * couples:2].set(receiver + passed)
    return tallies[jax.random.permutation(jax.random.fold_in(rng, 2), count)]


def centred(stream_key, shape, scale, bound, split=(), held_as=jnp.bfloat16):
    gain = block_scale(stream_key, shape, split, -0.22, 0.18) if split else 1.0
    entries = jax.random.normal(stream_key, shape, jnp.float32) * scale * gain
    return jnp.minimum(jnp.maximum(entries, -bound), bound).astype(held_as)


def setup_inputs(seed: int = 0) -> dict:
    arg_keys = jax.random.split(jax.random.key(seed), 17)
    tokens = centred(arg_keys[0], (SEQS, LEN, D), 1.0, 6.0, ((0, 4), (1, 2)))
    segments = jax.vmap(lambda own: jnp.searchsorted(jnp.cumsum(uneven_parts(own, max(LEN // 128, 4), LEN, LEN // 2, 2)), jnp.arange(LEN), side="right"))(jax.random.split(arg_keys[1], SEQS)).reshape((SEQS, LEN)).astype(jnp.int32)
    cotangent = centred(arg_keys[2], (SEQS, LEN, D), 1.0, 6.0, ((0, 4), (1, 2)))
    norm_gain = jnp.clip(1.0 + 0.1 * jax.random.normal(arg_keys[3], (D,), jnp.float32), 0.5, 1.5).astype(jnp.bfloat16)
    w_zx = centred(arg_keys[4], (D, 2, INNER), D ** -0.5, 0.21875, ((0, 4), (2, 4)))
    w_bc = centred(arg_keys[5], (D, 2 * STATE), D ** -0.5, 0.21875, ((0, 4),))
    w_dt = centred(arg_keys[6], (D, HEADS), D ** -0.5, 0.21875, ((0, 4), (1, 4)))
    conv_x = centred(arg_keys[7], (CONV, INNER), CONV ** -0.5, 3.0, ((1, 4),), jnp.float32)
    conv_x_bias = centred(arg_keys[8], (INNER,), 0.3, 1.5, ((0, 4),), jnp.float32)
    conv_bc = centred(arg_keys[9], (CONV, 2 * STATE), CONV ** -0.5, 3.0, (), jnp.float32)
    conv_bc_bias = centred(arg_keys[10], (2 * STATE,), 0.3, 1.5, (), jnp.float32)
    a_log = jnp.clip(-2.0 + 4.5 * jax.random.uniform(arg_keys[11], (HEADS,), jnp.float32) ** block_scale(arg_keys[11], (HEADS,), ((0, 4),), -0.2, 0.2), -2.0, 2.5)
    dt_bias = jnp.clip(-5.0 + 2.0 * jax.random.uniform(arg_keys[12], (HEADS,), jnp.float32) ** block_scale(arg_keys[12], (HEADS,), ((0, 4),), -0.2, 0.2), -5.0, -3.0)
    d_skip = jnp.clip(0.5 + 1.0 * jax.random.uniform(arg_keys[13], (HEADS,), jnp.float32) ** block_scale(arg_keys[13], (HEADS,), ((0, 4),), -0.2, 0.2), 0.5, 1.5)
    gate_gain = jnp.clip(1.0 + 0.1 * jax.random.normal(arg_keys[14], (INNER,), jnp.float32), 0.5, 1.5)
    w_out_t = centred(arg_keys[15], (D, INNER), INNER ** -0.5, 0.15625, ((0, 4), (1, 4)))
    return dict(tokens=tokens, segments=segments, cotangent=cotangent, norm_gain=norm_gain, w_zx=w_zx, w_bc=w_bc, w_dt=w_dt, conv_x=conv_x, conv_x_bias=conv_x_bias, conv_bc=conv_bc, conv_bc_bias=conv_bc_bias, a_log=a_log, dt_bias=dt_bias, d_skip=d_skip, gate_gain=gate_gain, w_out_t=w_out_t)


EPS = 1e-05
HIGH = lax.Precision.HIGHEST

@jax.custom_vjp
def low(v):
    return lax.optimization_barrier(v.astype(jnp.bfloat16)).astype(jnp.float32)

@jax.custom_vjp
def low_back(v):
    return v

def low_keep(v):
    return (low(v), None)

def low_pass(kept, grad):
    return (grad,)

def back_keep(v):
    return (v, None)

def back_low(kept, grad):
    return (low(grad),)
low.defvjp(low_keep, low_pass)
low_back.defvjp(back_keep, back_low)

def causal_ext(extended, weights, bias, seg_ext):
    width = weights.shape[0]
    span = extended.shape[0] - width + 1
    own = seg_ext[width - 1:]
    total = bias[None, :] + jnp.zeros((span, extended.shape[1]), extended.dtype)
    for k in range(width):
        piece = extended[width - 1 - k:width - 1 - k + span]
        same = (seg_ext[width - 1 - k:width - 1 - k + span] == own).astype(extended.dtype)
        total = total + weights[width - 1 - k][None, :] * piece * same[:, None]
    return total

def group_step(carry, pieces):
    state, prev = carry
    xh, bm, cm, decay_log, steps, seg = pieces
    length = xh.shape[0]
    cum = jnp.cumsum(decay_log, axis=0)
    order = jnp.arange(length)[:, None] >= jnp.arange(length)[None, :]
    tri = (order & (seg[:, None] == seg[None, :]))[:, :, None]
    diff = cum[:, None, :] - cum[None, :, :]
    decay = jnp.where(tri, jnp.exp(jnp.where(tri, diff, 0.0)), 0.0)
    scores = jnp.dot(cm, bm.T, precision=HIGH)
    mixing = scores[:, :, None] * decay * steps[None, :, :]
    out = jnp.einsum('tsh,shp->thp', mixing, xh, precision=HIGH)
    carry_on = (seg == prev).astype(cum.dtype)
    gate_t = jnp.exp(cum) * carry_on[:, None]
    out = out + gate_t[:, :, None] * jnp.einsum('tn,hpn->thp', cm, state, precision=HIGH)
    last = seg[-1]
    tail = jnp.exp(cum[-1][None, :] - cum) * (seg == last).astype(cum.dtype)[:, None] * steps
    new_state = gate_t[-1][:, None, None] * state + jnp.einsum('sh,shp,sn->hpn', tail, xh, bm, precision=HIGH)
    return ((new_state, last), out)

def piece_one(xc, bm, cm, dtr, dtb, alog, seg_loc, prev_id):
    span, inner = xc.shape
    heads = alog.shape[0]
    size = inner // heads
    steps = jax.nn.softplus(dtr + dtb[None, :])
    decay_log = -jnp.exp(alog)[None, :] * steps
    count = span // GROUP
    pieces = (xc.reshape(count, GROUP, heads, size), bm.reshape(count, GROUP, -1), cm.reshape(count, GROUP, -1), decay_log.reshape(count, GROUP, heads), steps.reshape(count, GROUP, heads), seg_loc.reshape(count, GROUP))
    init = (jnp.zeros((heads, size, bm.shape[1]), jnp.float32), prev_id)
    (state_end, last), outs = lax.scan(jax.checkpoint(group_step), init, pieces)
    cum = jnp.cumsum(decay_log, axis=0)
    gate_end = jnp.exp(cum[-1]) * (seg_loc[-1] == prev_id).astype(cum.dtype)
    return (outs.reshape(span, inner), state_end, gate_end, cum)

def layer(x, seg, params):
    ng, wzx, wbc, wdt, cx, cxb, cbc, cbcb, alog, dtb, dsk, gg, wout = params
    length = x.shape[0]
    r = lax.rsqrt(lax.optimization_barrier(jnp.mean(x * x, -1, keepdims=True)) + EPS)
    xn = low(x * r * ng)
    zx = low(low_back(jnp.einsum('td,dki->tki', xn, wzx, precision=HIGH)))
    z = zx[:, 0]
    xs = zx[:, 1]
    bc = low(jnp.dot(xn, wbc, precision=HIGH))
    dtr = low_back(jnp.dot(xn, wdt, precision=HIGH))
    seg_ext = jnp.concatenate([jnp.full((CONV - 1,), -1, jnp.int32), seg.astype(jnp.int32)])
    xs_ext = jnp.concatenate([jnp.zeros((CONV - 1, xs.shape[1]), xs.dtype), xs])
    bc_ext = jnp.concatenate([jnp.zeros((CONV - 1, bc.shape[1]), bc.dtype), bc])
    xc = low(jax.nn.silu(causal_ext(xs_ext, cx, cxb, seg_ext)))
    bcc = low(jax.nn.silu(causal_ext(bc_ext, cbc, cbcb, seg_ext)))
    bm = bcc[:, :STATE]
    cm = bcc[:, STATE:]
    ys = piece_one(xc, bm, cm, dtr, dtb, alog, seg.astype(jnp.int32), jnp.array(-1, jnp.int32))[0]
    y = ys + jnp.repeat(dsk, HEAD)[None, :] * xc
    yg = y * jax.nn.silu(z)
    r2 = lax.rsqrt(lax.optimization_barrier(jnp.mean(yg * yg, -1, keepdims=True)) + EPS)
    h = low(yg * r2 * gg)
    o = low_back(jnp.dot(h, wout.T, precision=HIGH))
    return x + o

def reference(tokens, segments, cotangent, norm_gain, w_zx, w_bc, w_dt, conv_x, conv_x_bias, conv_bc, conv_bc_bias, a_log, dt_bias, d_skip, gate_gain, w_out_t):
    params = tuple((p.astype(jnp.float32) for p in (norm_gain, w_zx, w_bc, w_dt, conv_x, conv_x_bias, conv_bc, conv_bc_bias, a_log, dt_bias, d_skip, gate_gain, w_out_t)))
    xf = tokens.astype(jnp.float32)

    def forward(inputs, weights):

        def one(pair):
            return layer(pair[0], pair[1], weights)
        return lax.map(jax.checkpoint(one), (inputs, segments))
    out, pull = jax.vjp(forward, xf, params)
    dx, grads = pull(cotangent.astype(jnp.float32))
    return (out.astype(jnp.bfloat16), dx.astype(jnp.bfloat16), grads[0], grads[1], grads[2], grads[3], grads[4], grads[5], grads[6], grads[7], grads[8], grads[9], grads[10], grads[11], grads[12])
```

```python
import functools
from types import SimpleNamespace

import jax
import jax.numpy as jnp
from jax import lax
from jax.experimental import pallas as pl
from jax.experimental.pallas import tpu as pltpu
from jax.sharding import PartitionSpec as P

EPS = 1e-05
Q = 128
LANES = 128
HP = 8
NEG = -1e30
VMEM_LIMIT = 60 << 20
F32 = jnp.float32
BF16 = jnp.bfloat16
MESH = pl.DeviceIdType.MESH
HIGH = lax.Precision.HIGHEST
COPIES = 176
SENDS = 72
C_DT, C_CUM, C_SEG, C_SAME, C_NEXT = 0, 8, 16, 17, 20


def nn(a, b, **kw):
    return lax.dot_general(a, b, (((1,), (0,)), ((), ())), preferred_element_type=F32, **kw)


def nt(a, b):
    return lax.dot_general(a, b, (((1,), (1,)), ((), ())), preferred_element_type=F32)


def iota(shape, dim):
    return lax.broadcasted_iota(jnp.int32, shape, dim)


def mult(value, by):
    return pl.multiple_of(value, by)


def fold(a):
    return jnp.sum(a.reshape(a.shape[0] // 8, 8, a.shape[1]), axis=0)


def sigmoid(v):
    return 0.5 * jnp.tanh(0.5 * v) + 0.5


def softplus(v):
    e = jnp.exp(-jnp.abs(v))
    w = 1.0 + e
    small = w == 1.0
    log1p = jnp.where(small, e, jnp.log(w) * e / jnp.where(small, 1.0, w - 1.0))
    return jnp.maximum(v, 0.0) + log1p

def body(g, r):
    d, c, t = lax.axis_index("dp"), lax.axis_index("context"), lax.axis_index("tensor")
    B, T, M, D, I, H, N = g.B, g.T, g.M, g.D, g.I, g.H, g.N
    NC = T // Q
    KX = I + 2 * N
    KW = 2 * I + 2 * N
    PAIRS = I // LANES
    DH = D // 2
    partner = (d, 1 - c, t)
    tensor_peer = lambda i: (d, c, jnp.bitwise_xor(t, i))
    dp_peer = lambda i: (lax.rem(d + i, g.dp), c, t)
    xb, yb = lax.rem(t, 2), lax.div(t, 2)
    XP, YP = tensor_peer(1), tensor_peer(2)
    used = [0]
    free = list(range(SENDS))
    slot = {}
    sent = []

    def remote(src, dst, device):
        at, out = used[0], free.pop(0)
        used[0] += 1
        cp = pltpu.make_async_remote_copy(
            src_ref=src,
            dst_ref=dst,
            send_sem=r.send.at[out],
            recv_sem=r.recv.at[at],
            device_id=device,
            device_id_type=MESH,
        )
        slot[id(cp)] = (out, cp)
        return cp

    def release(cp):
        free.append(slot[id(cp)][0])

    def send(src, dst, device):
        cp = remote(src, dst, device)
        cp.start()
        sent.append(cp)
        return cp

    def sweep(last):
        while len(sent) > last:
            cp = sent.pop(0)
            cp.wait_send()
            release(cp)

    bar = pltpu.get_barrier_semaphore()
    peers = [partner] + [tensor_peer(i) for i in range(1, g.tensor)]
    if g.ring:
        peers += [dp_peer(i) for i in range(1, g.dp)]
    for peer in peers:
        pl.semaphore_signal(bar, inc=1, device_id=peer, device_id_type=MESH)

    half_m = M // 2
    loads = []
    for k, (src, dst) in enumerate(((r.tokens_in, r.tokens), (r.cot_in, r.cot))):
        for q in range(2):
            rows = pl.ds(q * half_m, half_m)
            loads.append(pltpu.make_async_copy(src.at[rows], dst.at[rows], r.local.at[2 * k + q]))
            loads[-1].start()

    R = D // g.dp
    half = R // 2
    mine = pl.ds(mult(d * R, R), R) if g.ring else slice(0, D)
    r.w[mine, 2 * I : KW] = r.w_bc[...]
    r.w[mine, KW:] = r.w_out[...]
    pl.semaphore_wait(bar, len(peers))

    def gather_copies(cols):
        flows = []
        for s in range(g.dp - 1):
            for way in (1, -1):
                j = d - way * s
                to = d + way
                sends = (j >= 0) & (j < g.dp) & (to >= 0) & (to < g.dp)
                src_j = d - way * (s + 1)
                gets = (src_j >= 0) & (src_j < g.dp)
                jj = jnp.clip(j, 0, g.dp - 1)
                rows = pl.ds(mult(jj * R + c * half, half), half)
                go = remote(r.w.at[rows, cols], r.w.at[rows, cols], (jnp.clip(to, 0, g.dp - 1), c, t))
                kk = jnp.clip(src_j, 0, g.dp - 1)
                krows = pl.ds(mult(kk * R + c * half, half), half)
                side = remote(r.w.at[krows, cols], r.w.at[krows, cols], partner)
                flows.append((s, sends, gets, go, side))
        return flows

    def gather_send(flows, s):
        for at, sends, _, go, _ in flows:
            if at == s:
                pl.when(sends)(go.start)

    def gather_take(flows, s):
        for at, _, gets, go, side in flows:
            if at == s:

                @pl.when(gets)
                def _():
                    go.wait_recv()
                    side.start()

    def gather_end(flows):
        for _, sends, gets, go, side in flows:
            pl.when(gets)(side.wait_recv)
            pl.when(gets)(side.wait_send)
            pl.when(sends)(go.wait_send)
            release(go)
            release(side)

    if g.ring:
        dts = [send(r.wdt_own, r.wdt_in.at[i - 1], dp_peer(i)) for i in range(1, g.dp)]
        part_bc, part_z, part_x, part_o = [
            gather_copies(pl.ds(*a)) for a in ((2 * I, 2 * N), (0, I), (I, I), (KW, I))
        ]
        gather_send(part_bc, 0)
    r.w[mine, I : 2 * I] = r.w_zx[:, 1, :]
    if g.ring:
        gather_send(part_x, 0)
    r.w[mine, 0:I] = r.w_zx[:, 0, :]
    if g.ring:
        gather_send(part_z, 0)

    lanes8, row8 = iota((8, LANES), 1), iota((8, LANES), 0)
    alog, dtb = jnp.zeros((8, LANES), F32), jnp.zeros((8, LANES), F32)
    skip = jnp.zeros((1, I), F32)
    lanes_i = iota((1, I), 1)
    for h in range(H):
        alog = jnp.where(row8 == h, r.alog_in[h], alog)
        dtb = jnp.where(row8 == h, r.dtb_in[h], dtb)
        skip = jnp.where((lanes_i >= h * (I // H)) & (lanes_i < (h + 1) * (I // H)), r.skip_in[h], skip)
    r.rate[...] = -jnp.exp(alog)
    r.dtb[...] = dtb
    r.skip[...] = skip
    r.ggain[...] = r.ggain_in[...].reshape(1, I)
    r.gain[...] = r.gain_in[...].astype(F32).reshape(1, D)
    r.conv[0:4, 0:I] = r.conv_x[...]
    r.conv[0:4, I:] = r.conv_bc[...]
    r.conv[4:5, 0:I] = r.conv_xb[...].reshape(1, I)
    r.conv[4:5, I:] = r.conv_bcb[...].reshape(1, 2 * N)

    def norm(i, _):
        rows = pl.ds(mult(i * Q, Q), Q)
        x = r.tokens[rows].astype(F32)
        ratio = lax.rsqrt(jnp.sum(x * x, -1, keepdims=True) * (1.0 / D) + EPS)
        xn = (x * ratio * r.gain[...]).astype(BF16)
        r.xn[rows] = xn
        xf = xn.astype(F32)
        for k in range(D // LANES):
            cut = slice(k * LANES, (k + 1) * LANES)
            r.xnt[cut, rows] = xf[:, cut].T.astype(BF16)
        return 0

    def turn(i, _):
        rows = pl.ds(mult(i * Q, Q), Q)
        gf = r.cot[rows].astype(F32)
        for k in range(D // LANES):
            cut = slice(k * LANES, (k + 1) * LANES)
            r.gt[cut, rows] = gf[:, cut].T.astype(BF16)
        return 0

    def masks():
        lane, row = iota((8, Q), 1), iota((8, Q), 0)
        for b in range(B):
            s = jnp.concatenate([r.segments[b : b + 1, k * Q : (k + 1) * Q] for k in range(8)], 0).astype(F32)
            last = jnp.broadcast_to(s[:, Q - 1 :], (8, Q))
            prev = jnp.where(row == 0, -1.0, pltpu.roll(last, 1, 0))
            r.rowm[b, 0] = s
            for k in (1, 2, 3):
                a = pltpu.roll(s, k, 1)
                v = jnp.where(lane < k, pltpu.roll(a, 1, 0), a)
                hit = (v == s) & ((row > 0) | (lane >= k))
                r.rowm[b, k] = jnp.where(hit, 1.0, 0.0)
                a = pltpu.roll(s, Q - k, 1)
                v = jnp.where(lane >= Q - k, pltpu.roll(a, 7, 0), a)
                hit = (v == s) & ((row < 7) | (lane < Q - k))
                r.rowm[b, 3 + k] = jnp.where(hit, 1.0, 0.0)
            r.rowm[b, 7] = jnp.where(s == prev, 1.0, 0.0)
            r.rowm[b, 8] = jnp.where(s == last, 1.0, 0.0)

    def clear():
        r.taps[...] = jnp.zeros_like(r.taps)
        r.sums[...] = jnp.zeros_like(r.sums)
        r.heads[...] = jnp.zeros_like(r.heads)
        r.ddtr[HP:16] = jnp.zeros((16 - HP, M), BF16)
        for b in range(B):

            @pl.when(c == 0)
            def _():
                r.vext[b, 0:8] = jnp.zeros((8, KX), F32)
                r.state[b, 0] = jnp.zeros((N, I), F32)

            @pl.when(c == 1)
            def _():
                r.duext[b, T : T + 8] = jnp.zeros((8, KX), F32)
                r.dstate[b, NC] = jnp.zeros((N, I), F32)

    tri = jnp.where(iota((Q, Q), 0) <= iota((Q, Q), 1), 1.0, 0.0)
    lane = iota((Q, LANES), 1)
    left = lane < LANES // 2

    def spread(cols, first):
        return jnp.concatenate(
            [
                jnp.where(left, cols[:, first + 2 * p : first + 2 * p + 1], cols[:, first + 2 * p + 1 : first + 2 * p + 2])
                for p in range(PAIRS)
            ],
            1,
        )

    def time_steps():
        wdt = jnp.zeros((H, D), F32)
        if g.ring:
            for i in range(g.dp):
                if i:
                    dts[i - 1].wait_recv()
                part = r.wdt_own[...] if i == 0 else r.wdt_in[i - 1]
                j = lax.rem(d - i + g.dp, g.dp)
                hit = iota((R, D), 1) == iota((R, D), 0) + j * R
                wdt = wdt + nn(part, jnp.where(hit, 1.0, 0.0).astype(BF16))
        else:
            wdt = r.wdt_own[...].astype(F32)
        r.wdt[...] = jnp.concatenate([wdt, jnp.zeros((LANES - H, D), F32)], 0).astype(BF16)
        r.dtr[...] = nt(r.wdt[0:16], r.xn[...])[0:HP]

    def prep(b, lo, hi):
        def one(j, _):
            rows = pl.ds(mult(b * T + j * Q, Q), Q)
            at = c * NC + j
            mask = lambda k: r.rowm[b, k, pl.ds(at, 1)]
            dt = softplus(r.dtr[:, rows] + r.dtb[...])
            cum = nn(r.rate[...] * dt, tri, precision=HIGH)
            gate = jnp.exp(cum) * mask(7)
            tail = jnp.exp(cum[:, Q - 1 :] - cum) * mask(8)
            r.dt[:, rows] = dt
            r.cum[:, rows] = cum
            table = jnp.concatenate([dt, cum] + [mask(k) for k in range(7)] + [jnp.zeros((1, Q), F32), gate, tail, jnp.zeros((Q - 40, Q), F32)], 0)
            cols = table.T
            r.cols[rows] = cols
            r.dt_wide[rows] = spread(cols, C_DT)
            r.gate_wide[rows] = spread(cols, 24)
            r.tail_wide[rows] = spread(cols, 32)
            return 0

        lax.fori_loop(lo, hi, one, 0)

    MB = M // Q

    def relay(part, at):
        gather_take(part, at)
        gather_send(part, at + 1)

    loads[0].wait()
    lax.fori_loop(0, MB // 2, norm, 0)
    loads[1].wait()
    lax.fori_loop(MB // 2, MB, norm, 0)
    if g.ring:
        relay(part_bc, 0)
    masks()
    clear()
    time_steps()
    if g.ring:
        relay(part_x, 0)
    prep(0, 0, NC // 2)
    if g.ring:
        relay(part_bc, 1)
        relay(part_z, 0)
    prep(0, NC // 2, NC)
    if g.ring:
        relay(part_x, 1)
        gather_send(part_o, 0)
    prep(1, 0, NC // 2)
    if g.ring:
        relay(part_bc, 2)
        relay(part_z, 1)
    prep(1, NC // 2, NC)
    loads[2].wait()
    loads[3].wait()
    if g.ring:
        relay(part_x, 2)
        gather_end(part_bc)
        gather_end(part_x)

    def project(b, first, last):
        rows = slice(b * T, (b + 1) * T)
        ext = slice(8, 8 + T)
        xn = r.xn[rows]
        low = lambda a: a.astype(BF16).astype(F32)
        for lo in range(first, last, 2 * LANES):
            hi = min(lo + 2 * LANES, last)
            res = nn(xn, r.w[:, lo:hi])
            if hi <= I:
                r.z[rows, lo:hi] = res.astype(BF16)
            else:
                r.vext[b, ext, lo - I : hi - I] = low(res)

    def conv(b):
        def one(j, _):
            base = mult(j * Q, Q)
            rows = pl.ds(mult(b * T + j * Q, Q), Q)
            cols = r.cols[rows]
            same = [cols[:, C_SAME + k : C_SAME + k + 1] for k in range(3)]
            outs = []
            for p in range(KX // LANES):
                cut = slice(p * LANES, (p + 1) * LANES)
                blk = r.vext[b, pl.ds(base, Q + 8), cut]
                u = r.conv[4:5, cut] + r.conv[3:4, cut] * blk[8:]
                for k in (1, 2, 3):
                    u = u + r.conv[3 - k : 4 - k, cut] * blk[8 - k : Q + 8 - k] * same[k - 1]
                sg = sigmoid(u)
                r.dsilu[rows, cut] = sg * (1.0 + u * (1.0 - sg))
                outs.append((u * sg).astype(BF16))
            for p in range(PAIRS):
                cut = slice(p * LANES, (p + 1) * LANES)
                r.xc[rows, cut] = outs[p]
                xdt = outs[p].astype(F32) * r.dt_wide[rows, cut]
                r.xdt[rows, cut] = xdt.astype(BF16)
                r.xt[rows, cut] = (xdt * r.tail_wide[rows, cut]).astype(BF16)
            bm, cm = outs[PAIRS], outs[PAIRS + 1]
            r.bm[rows] = bm
            r.cm[rows] = cm
            bt = bm.astype(F32).T.astype(BF16)
            r.ct[rows] = cm.astype(F32).T.astype(BF16)
            r.own_state[b, j] = nn(bt, r.xt[rows])
            return 0

        lax.fori_loop(0, NC, one, 0)

    def end_gate(b, j):
        return r.gate_wide[b * T + (j + 1) * Q - 1 : b * T + (j + 1) * Q]

    def chain(b):
        for j in range(NC):
            r.state[b, j + 1] = end_gate(b, j) * r.state[b, j] + r.own_state[b, j]

    def inner(b):
        def one(j, _):
            rows = pl.ds(mult(b * T + j * Q, Q), Q)
            cols = r.cols[rows]
            cum = r.cum[:, rows]
            seg = r.rowm[b, 0, pl.ds(c * NC + j, 1)]
            keep = (cols[:, C_SEG : C_SEG + 1] == seg) & (iota((Q, Q), 0) >= iota((Q, Q), 1))
            scores = nt(r.cm[rows], r.bm[rows])
            for p in range(PAIRS):
                cut = slice(p * LANES, (p + 1) * LANES)
                x = r.xdt[rows, cut]
                mix = []
                for q in range(2):
                    h = 2 * p + q
                    diff = cols[:, C_CUM + h : C_CUM + h + 1] - cum[h : h + 1]
                    mix.append((scores * jnp.exp(jnp.where(keep, diff, NEG))).astype(BF16))
                zero = jnp.zeros_like(x)
                both = jnp.concatenate([jnp.where(left, x, zero), jnp.where(left, zero, x)], 0)
                r.ys[rows, cut] = nn(jnp.concatenate(mix, 1), both)
            return 0

        lax.fori_loop(0, NC, one, 0)

    def as_row(a):
        return jnp.broadcast_to(jnp.sum(a, -1, keepdims=True), (Q, LANES)).T[0:8]

    def as_column(own, far, at):
        total = own[:, at]
        for i in range(g.tensor - 1):
            total = total + far[i, :, at]
        return jnp.concatenate([total, jnp.zeros((Q - 8, Q), F32)], 0).T

    def outer(b):
        def one(j, _):
            rows = pl.ds(mult(b * T + j * Q, Q), Q)
            carried = nn(r.cm[rows], r.state[b, j].astype(BF16))
            squares = jnp.zeros((Q, LANES), F32)
            for p in range(PAIRS):
                cut = slice(p * LANES, (p + 1) * LANES)
                ys = r.ys[rows, cut] + r.gate_wide[rows, cut] * carried[:, cut]
                r.ys[rows, cut] = ys
                y = ys + r.skip[:, cut] * r.xc[rows, cut].astype(F32)
                z = r.z[rows, cut].astype(F32)
                yg = y * z * sigmoid(z)
                r.yg[rows, cut] = yg
                squares = squares + yg * yg
            r.norms[b, :, pl.ds(mult(j * Q, Q), Q)] = as_row(squares)
            return 0

        lax.fori_loop(0, NC, one, 0)

    def dhidden(b):
        rows = slice(b * T, (b + 1) * T)
        g_out = r.cot[rows]
        for k in range(PAIRS):
            cut = slice(k * LANES, (k + 1) * LANES)
            r.dh[rows, cut] = nn(g_out, r.w[:, KW + k * LANES : KW + (k + 1) * LANES])

    inner_total = I * g.tensor

    def hidden(b):
        def one(j, _):
            rows = pl.ds(mult(b * T + j * Q, Q), Q)
            at = pl.ds(mult(j * Q, Q), Q)
            ratio = lax.rsqrt(as_column(r.norms.at[b], r.norms_in.at[b], at) * (1.0 / inner_total) + EPS)
            r.r2[rows] = ratio
            inners = jnp.zeros((Q, LANES), F32)
            for p in range(PAIRS):
                cut = slice(p * LANES, (p + 1) * LANES)
                scaled = r.yg[rows, cut] * r.ggain[:, cut]
                r.h[rows, cut] = (scaled * ratio[:, 0:1]).astype(BF16)
                inners = inners + scaled * r.dh[rows, cut]
            r.inners[b, :, at] = as_row(inners)
            return 0

        lax.fori_loop(0, NC, one, 0)

    def gated(b):
        def one(j, _):
            rows = pl.ds(mult(b * T + j * Q, Q), Q)
            at = pl.ds(mult(j * Q, Q), Q)
            r2 = r.r2[rows, 0:1]
            cols = as_column(r.inners.at[b], r.inners_in.at[b], at)
            pull = r2 * r2 * r2 * cols[:, 0:1] * (1.0 / inner_total)
            for p in range(PAIRS):
                cut = slice(p * LANES, (p + 1) * LANES)
                yg = r.yg[rows, cut]
                gain = r.ggain[:, cut]
                dh = r.dh[rows, cut]
                z = r.z[rows, cut].astype(F32)
                xc = r.xc[rows, cut].astype(F32)
                y = r.ys[rows, cut] + r.skip[:, cut] * xc
                sg = sigmoid(z)
                r.sums[0, :, cut] += fold(dh * yg * r2)
                dyg = gain * dh * r2 - yg * pull
                dy = dyg * z * sg
                r.dcat[rows, cut] = (dyg * y * sg * (1.0 + z * (1.0 - sg))).astype(BF16)
                r.sums[1, :, cut] += fold(dy * xc)
                r.dy[rows, cut] = dy.astype(BF16)
                r.dyg[rows, cut] = (dy * r.gate_wide[rows, cut]).astype(BF16)
            r.own_dstate[b, j] = nn(r.ct[rows], r.dyg[rows])
            return 0

        lax.fori_loop(0, NC, one, 0)

    def part_out(b):
        rows = slice(b * T, (b + 1) * T)
        h = r.h[rows]
        for k in range(D // (2 * LANES)):
            cut = slice(k * 2 * LANES, (k + 1) * 2 * LANES)
            res = nt(h, r.w[cut, KW : KW + I]).astype(BF16)
            r.po[b, :, :, :, cut] = res.reshape(2, 2, T // 4, 2 * LANES)

    COLS = (pl.ds(0, DH), pl.ds(DH, DH))
    flip = lambda i: jnp.bitwise_xor(t, i)

    def quarter(base, size, q):
        return pl.ds(mult(base + q * (size // g.tensor), size // g.tensor), size // g.tensor)

    class Sum:
        def __init__(self, src, base, size, in1, in2, mid):
            self.src, self.base, self.size = src, base, size
            self.in1, self.in2, self.mid = in1, in2, mid
            self.rows = lambda q: quarter(base, size, q)

        def first(self):
            src, in1 = self.src, self.in1
            self.a = send(src.at[:, 1 - xb, :, COLS[0]], in1.at[0], XP)
            self.c = send(src.at[1 - yb, :, :, COLS[1]], in1.at[1], YP)

        def second(self):
            src, in1, in2, mid = self.src, self.in1, self.in2, self.mid
            self.a.wait_recv()
            self.c.wait_recv()
            mid[0] = (src[1 - yb, xb, :, 0:DH].astype(F32) + in1[0, 1 - yb].astype(F32)).astype(BF16)
            mid[1] = (src[yb, 1 - xb, :, DH:].astype(F32) + in1[1, 1 - xb].astype(F32)).astype(BF16)
            self.e = [send(mid.at[0], in2.at[0], YP), send(mid.at[1], in2.at[1], XP)]

        def total(self):
            src, in1, in2 = self.src, self.in1, self.in2
            for cp in self.e:
                cp.wait_recv()
            mine = src[yb, xb].astype(F32)
            low = mine[:, 0:DH] + in1[0, yb].astype(F32) + in2[0].astype(F32)
            high = mine[:, DH:] + in1[1, xb].astype(F32) + in2[1].astype(F32)
            return jnp.concatenate([low, high], 1)

    class Spread:
        def __init__(self, dst, base, size):
            self.dst, self.base, self.size = dst, base, size

        def to(self, q, half_, device):
            at = self.dst.at[quarter(self.base, self.size, q), COLS[half_]]
            return send(at, at, device)

        def first(self):
            self.x0, self.y1 = self.to(t, 0, XP), self.to(t, 1, YP)
            self.x1, self.y0 = self.to(t, 1, XP), self.to(t, 0, YP)

        def second(self):
            self.x0.wait_recv()
            self.f0 = self.to(flip(1), 0, YP)
            self.y1.wait_recv()
            self.f1 = self.to(flip(2), 1, XP)

        def last(self):
            for cp in (self.x1, self.y0, self.f0, self.f1):
                cp.wait_recv()

    def back_chain(b):
        for j in reversed(range(NC)):
            r.dstate[b, j] = end_gate(b, j) * r.dstate[b, j + 1] + r.own_dstate[b, j]

    def back_inner(b):
        def one(j, _):
            rows = pl.ds(mult(b * T + j * Q, Q), Q)
            cols = r.cols[rows]
            cum = r.cum[:, rows]
            seg = r.rowm[b, 0, pl.ds(c * NC + j, 1)]
            keep = (cols[:, C_SEG : C_SEG + 1] == seg) & (iota((Q, Q), 1) >= iota((Q, Q), 0))
            bm, cm = r.bm[rows], r.cm[rows]
            scores = nt(bm, cm)
            dscores = jnp.zeros((Q, Q), F32)
            for p in range(PAIRS):
                cut = slice(p * LANES, (p + 1) * LANES)
                x, dy = r.xdt[rows, cut], r.dy[rows, cut]
                zero = jnp.zeros_like(x)
                dmix = nt(jnp.concatenate([jnp.where(left, x, zero), jnp.where(left, zero, x)], 0), dy)
                mix = []
                for q in range(2):
                    h = 2 * p + q
                    diff = cum[h : h + 1] - cols[:, C_CUM + h : C_CUM + h + 1]
                    decay = jnp.exp(jnp.where(keep, diff, NEG))
                    mix.append((scores * decay).astype(BF16))
                    dscores = dscores + dmix[q * Q : (q + 1) * Q] * decay
                both = jnp.concatenate([jnp.where(left, dy, zero), jnp.where(left, zero, dy)], 0)
                r.dxdt[rows, cut] = nn(jnp.concatenate(mix, 1), both)
            r.dbc[rows, 0:N] = nn(dscores.astype(BF16), cm)
            r.dbc[rows, N : 2 * N] = nn(dscores.T.astype(BF16), bm)
            return 0

        lax.fori_loop(0, NC, one, 0)

    own_head = jnp.where(iota((16, I), 1) // (I // H) == iota((16, I), 0), 1.0, 0.0).astype(BF16)

    def by_head(a):
        return nt(own_head, a.astype(BF16))[0:HP]

    later = jnp.where(iota((Q, Q), 0) >= iota((Q, Q), 1), 1.0, 0.0)

    def back_outer(b):
        def one(j, _):
            base = mult(j * Q, Q)
            rows = pl.ds(mult(b * T + j * Q, Q), Q)
            cols = r.cols[rows]
            dnext = r.dstate[b, j + 1]
            dlow = dnext.astype(BF16)
            xt = r.xt[rows]
            tail = nn(r.bm[rows], dlow)
            dxs = []
            prods = [[], []]
            for p in range(PAIRS):
                cut = slice(p * LANES, (p + 1) * LANES)
                v = r.dxdt[rows, cut] + r.tail_wide[rows, cut] * tail[:, cut]
                dy = r.dy[rows, cut].astype(F32)
                prods[0].append(dy * r.ys[rows, cut] - r.xdt[rows, cut].astype(F32) * v)
                prods[1].append(r.xc[rows, cut].astype(F32) * v)
                dxs.append(v * r.dt_wide[rows, cut] + r.skip[:, cut] * dy)
            dxs.append(r.dbc[rows, 0:N] + nt(xt, dlow))
            dxs.append(r.dbc[rows, N : 2 * N] + nt(r.dyg[rows], r.state[b, j].astype(BF16)))
            pull, push = [jnp.concatenate(a, 1) for a in prods]
            high = pull.astype(BF16).astype(F32)
            dcum = by_head(high) + by_head(pull - high)
            ddt = by_head(push)
            ends = jnp.sum(by_head(dnext * r.state[b, j + 1]), -1, keepdims=True)
            dcum = dcum + jnp.where(iota((HP, Q), 1) == Q - 1, ends, 0.0)
            dla = nn(dcum, later, precision=HIGH)
            rate = r.rate[...]
            dt = r.dt[:, rows]
            ddtr = (ddt + dla * rate) * sigmoid(r.dtr[:, rows] + r.dtb[...])
            r.heads[0] += dla * rate * dt
            r.heads[1] += ddtr
            r.ddtr[0:HP, rows] = ddtr.astype(BF16)
            for p in range(KX // LANES):
                cut = slice(p * LANES, (p + 1) * LANES)
                r.duext[b, pl.ds(base, Q), cut] = dxs[p] * r.dsilu[rows, cut]
            return 0

        lax.fori_loop(0, NC, one, 0)

    def back_conv(b, lo, hi):
        def one(j, _):
            base = mult(j * Q, Q)
            rows = pl.ds(mult(b * T + j * Q, Q), Q)
            cols = r.cols[rows]
            for p in range(KX // LANES):
                cut = slice(p * LANES, (p + 1) * LANES)
                blk = r.duext[b, pl.ds(base, Q + 8), cut]
                v = r.vext[b, pl.ds(mult(base + 8, 8), Q), cut]
                du = blk[0:Q]
                r.taps[4, :, cut] += fold(du)
                r.taps[3, :, cut] += fold(v * du)
                dv = r.conv[3:4, cut] * du
                for k in (1, 2, 3):
                    du = blk[k : Q + k] * cols[:, C_NEXT + k - 1 : C_NEXT + k]
                    r.taps[3 - k, :, cut] += fold(v * du)
                    dv = dv + r.conv[3 - k : 4 - k, cut] * du
                r.dcat[rows, I + p * LANES : I + (p + 1) * LANES] = dv.astype(BF16)
            return 0

        lax.fori_loop(lo, hi, one, 0)

    def part_dxn(at, base, size):
        rows = slice(base, base + size)
        dcat = r.dcat[rows]
        ddtr = jnp.concatenate([r.ddtr[0:HP, rows].astype(F32), jnp.zeros((LANES - HP, size), F32)], 0).T.astype(BF16)
        for k in range(D // (2 * LANES)):
            cut = slice(k * 2 * LANES, (k + 1) * 2 * LANES)
            res = nt(dcat, r.w[cut, 0:KW]) + nn(ddtr, r.wdt[:, cut])
            r.dxp[at, :, :, :, cut] = res.astype(BF16).reshape(2, 2, size // 4, 2 * LANES)

    def finish_out(s):
        rows = s.rows(t)
        r.out[rows] = (r.tokens[rows].astype(F32) + s.total()).astype(BF16)

    def finish_dx(s):
        rows = s.rows(t)
        dxn = s.total()
        x = r.tokens[rows].astype(F32)
        ratio = lax.rsqrt(jnp.sum(x * x, -1, keepdims=True) * (1.0 / D) + EPS)
        scaled = r.gain[...] * dxn
        dot = jnp.sum(scaled * x, -1, keepdims=True) * (1.0 / D)
        dx = ratio * scaled - x * (ratio * ratio * ratio * dot)
        r.gtok[rows] = (r.cot[rows].astype(F32) + dx).astype(BF16)
        return fold(dxn * x * ratio)

    HR = R // 2 if g.ring else R
    AT_Z, AT_O, AT_BC, AT_X = 0, I, 2 * I, 2 * I + 2 * N

    def weight_grad(first, width, left_ref, right_ref, column):
        for lo in range(0, width, 2 * LANES):
            wide = min(2 * LANES, width - lo)
            res = nn(left_ref[...], right_ref[:, column + lo : column + lo + wide])
            res = res.astype(BF16)
            if g.ring:
                r.dw[:, :, :, first + lo : first + lo + wide] = res.reshape(g.dp, 2, HR, wide)
            else:
                r.dw[:, first + lo : first + lo + wide] = res

    class Share:
        def __init__(self, first, width):
            self.cut, self.at = slice(first, first + width), pl.ds(first, width)

        def to_partner(self):
            self.pair = send(r.dw.at[:, 1 - c, :, self.at], r.dw_pair.at[:, :, self.at], partner)

        def over_dp(self):
            self.pair.wait_recv()
            for j in range(g.dp):
                both = r.dw[j, c, :, self.cut].astype(F32) + r.dw_pair[j, :, self.cut].astype(F32)
                r.dw_chip[j, :, self.cut] = both.astype(BF16)
            self.far = []
            for i in range(1, g.dp):
                j = lax.rem(d + i, g.dp)
                self.far.append(send(r.dw_chip.at[j, :, self.at], r.dw_in.at[i - 1, :, self.at], dp_peer(i)))

        def total(self):
            for cp in self.far:
                cp.wait_recv()
            total = r.dw_chip[d, :, self.cut].astype(F32)
            for i in range(g.dp - 1):
                total = total + r.dw_in[i, :, self.cut].astype(F32)
            return total

    one_row = lambda a: jnp.sum(a, axis=0, keepdims=True)

    def exchange(src, dst, devices):
        return [send(src, dst.at[i], device) for i, device in enumerate(devices)]

    def plus(src, dst, cps):
        for cp in cps:
            cp.wait_recv()
        total = src[...]
        for i in range(len(cps)):
            total = total + dst[i]
        return total

    over_tensor = [tensor_peer(i) for i in range(1, g.tensor)]
    over_line = [dp_peer(i) for i in range(1, g.dp)]

    halo = [remote(r.vext.at[b, pl.ds(T, 8)], r.vext.at[b, pl.ds(0, 8)], partner) for b in range(B)]
    states = [remote(r.state.at[b, NC], r.state.at[b, 0], partner) for b in range(B)]
    dstates = [remote(r.dstate.at[b, 0], r.dstate.at[b, NC], partner) for b in range(B)]
    du_rims = [remote(r.duext.at[b, pl.ds(0, 8)], r.duext.at[b, pl.ds(T, 8)], partner) for b in range(B)]
    HT = T // 2
    sum_out = [Sum(r.po.at[b], b * T, T, r.po_in1.at[b], r.po_in2.at[b], r.po_mid.at[b]) for b in range(B)]
    spread_out = [Spread(r.out, b * T, T) for b in range(B)]
    pieces = [b * T + h * HT for b in range(B) for h in (1, 0)]
    sum_dx = [Sum(r.dxp.at[i], a, HT, r.dx_in1.at[i], r.dx_in2.at[i], r.dx_mid.at[i]) for i, a in enumerate(pieces)]
    spread_dx = [Spread(r.gtok, a, HT) for a in pieces]
    norms, inners = [None] * B, [None] * B

    def start_forward(b):
        pl.when(c == 1)(halo[b].wait_recv)
        conv(b)

        @pl.when(c == 0)
        def _():
            chain(b)
            states[b].start()

    def end_forward(b):
        @pl.when(c == 1)
        def _():
            states[b].wait_recv()
            chain(b)

        outer(b)
        norms[b] = exchange(r.norms.at[b], r.norms_in.at[b], over_tensor)

    def out_part(b):
        for cp in norms[b]:
            cp.wait_recv()
        hidden(b)
        inners[b] = exchange(r.inners.at[b], r.inners_in.at[b], over_tensor)
        part_out(b)
        sum_out[b].first()

    def start_backward(b):
        for cp in inners[b]:
            cp.wait_recv()
        gated(b)

        @pl.when(c == 1)
        def _():
            back_chain(b)
            dstates[b].start()

    def end_backward(b):
        @pl.when(c == 0)
        def _():
            dstates[b].wait_recv()
            back_chain(b)

        back_outer(b)
        pl.when(c == 1)(du_rims[b].start)

    def dx_part(b, h):
        if h:
            pl.when(c == 0)(du_rims[b].wait_recv)
        back_conv(b, h * NC // 2, (h + 1) * NC // 2)
        at = 2 * b + 1 - h
        part_dxn(at, b * T + h * HT, HT)
        sum_dx[at].first()

    assert B == 2
    project(0, I, KW)
    pl.when(c == 0)(halo[0].start)
    if g.ring:
        relay(part_o, 0)
    start_forward(0)
    if g.ring:
        relay(part_z, 2)
        relay(part_o, 1)
    project(1, I, KW)
    pl.when(c == 0)(halo[1].start)
    inner(0)
    if g.ring:
        gather_end(part_z)
    project(0, 0, I)
    end_forward(0)
    if g.ring:
        relay(part_o, 2)
        gather_end(part_o)
    start_forward(1)
    dhidden(0)
    out_part(0)
    inner(1)
    project(1, 0, I)
    end_forward(1)
    dhidden(1)
    start_backward(0)
    out_part(1)
    sum_out[0].second()
    back_inner(0)
    start_backward(1)
    end_backward(0)
    sum_out[1].second()
    dx_part(0, 1)
    finish_out(sum_out[0])
    spread_out[0].first()
    dx_part(0, 0)
    early = Share(AT_Z, 2 * I)
    weight_grad(AT_Z, I, r.xnt, r.dcat, 0)
    lax.fori_loop(0, MB, turn, 0)
    weight_grad(AT_O, I, r.gt, r.h, 0)
    if g.ring:
        early.to_partner()
    back_inner(1)
    sum_dx[0].second()
    finish_out(sum_out[1])
    sum_dx[1].second()
    sweep(24)
    spread_out[1].first()
    end_backward(1)
    if g.ring:
        early.over_dp()
    gain_part = finish_dx(sum_dx[0])
    dx_part(1, 1)
    spread_out[0].second()
    gain_part = gain_part + finish_dx(sum_dx[1])
    dx_part(1, 0)
    spread_dx[0].first()
    spread_out[1].second()
    spread_dx[1].first()
    late_bc, late_x = Share(AT_BC, 2 * N), Share(AT_X, I)
    weight_grad(AT_BC, 2 * N, r.xnt, r.dcat, 2 * I)
    if g.ring:
        late_bc.to_partner()
    sum_dx[2].second()
    weight_grad(AT_X, I, r.xnt, r.dcat, I)
    if g.ring:
        late_x.to_partner()
        late_bc.over_dp()
    sum_dx[3].second()
    spread_dx[0].second()
    if g.ring:
        late_x.over_dp()
    sweep(24)
    row = iota((8, D), 0)
    by_lane = iota((8, D), 1)
    small = jnp.zeros((8, D), F32)
    pad = lambda a: jnp.concatenate([a, jnp.zeros((1, D - a.shape[1]), F32)], 1)
    for k in range(5):
        small = jnp.where(row == k, pad(one_row(r.taps[k])), small)
    small = jnp.where(row == 5, pad(one_row(r.sums[0])), small)
    small = jnp.where(row == 6, pad(one_row(r.sums[1])), small)
    small = jnp.where((row < H) & (by_lane == KX), jnp.sum(r.heads[0], -1, keepdims=True), small)
    small = jnp.where((row < H) & (by_lane == KX + 1), jnp.sum(r.heads[1], -1, keepdims=True), small)
    r.small[0:8] = small
    r.small[8:16] = nn(r.ddtr[...], r.xn[...])[0:8]
    if g.ring:
        pair = exchange(r.small, r.small_pair, [partner])
    gain_part = gain_part + finish_dx(sum_dx[2])
    spread_dx[2].first()
    spread_dx[1].second()
    gain_part = one_row(gain_part + finish_dx(sum_dx[3]))
    r.norm_own[...] = gain_part
    if g.ring:
        norm_t = exchange(r.norm_own, r.norm_t, over_tensor)
    spread_dx[3].first()
    if not g.ring:
        r.small_out[...] = r.small[...]
        r.small_out[7:8] = gain_part
        spread_dx[2].second()
        spread_dx[3].second()
    else:
        r.small_chip[...] = plus(r.small, r.small_pair, pair)
        line = exchange(r.small_chip, r.small_in, over_line)
        total = early.total()
        r.g_zx[:, 0:I] = total[:, 0:I]
        r.g_out[...] = total[:, I:]
        spread_dx[2].second()
        r.norm_plane[...] = plus(r.norm_own, r.norm_t, norm_t)
        norm_pair = exchange(r.norm_plane, r.norm_pair, [partner])
        total = plus(r.small_chip, r.small_in, line)
        r.small_dp[...] = total[0:8]
        plane = exchange(r.small_dp, r.small_t, over_tensor)
        r.norm_chip[...] = plus(r.norm_plane, r.norm_pair, norm_pair)
        norm_line = exchange(r.norm_chip, r.norm_in, over_line)
        r.bc_own[...] = late_bc.total()
        bc = exchange(r.bc_own, r.bc_in, over_tensor)
        spread_dx[3].second()
        r.g_zx[:, I:] = late_x.total()
        every = plus(r.small_dp, r.small_t, plane)
        shared = (row < 5) & (by_lane >= I) & (by_lane < KX)
        r.small_out[0:8] = jnp.where(shared, every, total[0:8])
        r.small_out[8:16] = total[8:16]
        r.small_out[7:8] = plus(r.norm_chip, r.norm_in, norm_line)
        r.g_bc[...] = plus(r.bc_own, r.bc_in, bc)

    for s in spread_out + spread_dx:
        s.last()
    sweep(0)
    for b in range(B):

        @pl.when(c == 0)
        def _():
            halo[b].wait_send()
            states[b].wait_send()

        @pl.when(c == 1)
        def _():
            dstates[b].wait_send()
            du_rims[b].wait_send()
    assert used[0] <= COPIES


def hand_out(g, r):
    I, H, KX = g.I, g.H, g.I + 2 * g.N
    copies = [
        (r.out_v, r.out),
        (r.gtok_v, r.gtok),
        (r.zx_v.at[:, pl.ds(0, I)], r.g_zx.at[:, 0, :]),
        (r.zx_v.at[:, pl.ds(I, I)], r.g_zx.at[:, 1, :]),
        (r.bc, r.g_bc),
        (r.wo, r.g_out),
    ]
    copies = [pltpu.make_async_copy(a, b, r.sem.at[k]) for k, (a, b) in enumerate(copies)]
    fetch = [pltpu.make_async_copy(a, b, r.sem.at[6 + k]) for k, (a, b) in enumerate(((r.bc_v, r.bc), (r.wo_v, r.wo)))]
    for cp in fetch + copies[:4]:
        cp.start()
    for k in range(2):
        fetch[k].wait()
        copies[4 + k].start()
    s = r.small_v[...]
    r.g_norm[...] = s[7]
    r.g_cx[...] = s[0:4, 0:I]
    r.g_cxb[...] = s[4, 0:I]
    r.g_cbc[...] = s[0:4, I:KX]
    r.g_cbcb[...] = s[4, I:KX]
    cols = s[0:H, KX : KX + LANES]
    ends = jnp.concatenate([cols, jnp.zeros((LANES - H, LANES), F32)], 0).T
    r.g_alog[...] = ends[0, 0:H]
    r.g_dtb[...] = ends[1, 0:H]
    r.g_gain[...] = s[5, 0:I]
    lanes = iota((LANES, I), 1) // (I // H)
    mine = jnp.where(lanes == iota((LANES, I), 0), jnp.broadcast_to(s[6:7, 0:I], (LANES, I)), 0.0)
    skips = jnp.broadcast_to(jnp.sum(mine, -1, keepdims=True), (LANES, LANES)).T
    r.g_skip[...] = skips[0, 0:H]
    rows = r.g_dt.shape[1]
    at = lax.axis_index("dp") * 2 + lax.axis_index("context")
    picked = jnp.zeros((8, rows), F32)
    for k in range(g.D // rows):
        picked = jnp.where(at == k, s[8:16, k * rows : (k + 1) * rows], picked)
    r.g_dt[...] = picked[0:H]
    for cp in copies:
        cp.wait()


def per_device(
    sizes,
    tokens,
    segments,
    cotangent,
    norm_gain,
    w_zx,
    w_bc,
    w_dt,
    conv_x,
    conv_x_bias,
    conv_bc,
    conv_bc_bias,
    a_log,
    dt_bias,
    d_skip,
    gate_gain,
    w_out_t,
):
    dp, context, tensor = sizes
    B, T, D = tokens.shape
    I = conv_x.shape[1]
    N = conv_bc.shape[1] // 2
    H = a_log.shape[0]
    M = B * T
    L = segments.shape[1]
    R = w_zx.shape[0]
    KX, KW = I + 2 * N, 2 * I + 2 * N
    W = KW + I
    NC = T // Q
    ring = dp == 4 and R % 32 == 0
    assert context == 2 and tensor == 4 and L == 8 * Q and I // H == 64 and H <= HP and I % LANES == 0
    g = SimpleNamespace(B=B, T=T, M=M, D=D, I=I, H=H, N=N, dp=dp, tensor=tensor, ring=ring)

    wdt_own = w_dt.T
    if not ring:
        w_zx, w_bc, w_out_t = [lax.all_gather(a, "dp", axis=0, tiled=True) for a in (w_zx, w_bc, w_out_t)]
        wdt_own = lax.all_gather(w_dt, "dp", axis=0, tiled=True).T
    vmem, smem, anywhere = [pl.BlockSpec(memory_space=m) for m in (pltpu.VMEM, pltpu.SMEM, pl.ANY)]
    ins = dict(
        tokens_in=(tokens.reshape(M, D), anywhere),
        cot_in=(cotangent.reshape(M, D), anywhere),
        segments=(segments, vmem),
        gain_in=(norm_gain, vmem),
        w_zx=(w_zx, vmem),
        w_bc=(w_bc, vmem),
        w_out=(w_out_t, vmem),
        wdt_own=(wdt_own, vmem),
        conv_x=(conv_x, vmem),
        conv_xb=(conv_x_bias, vmem),
        conv_bc=(conv_bc, vmem),
        conv_bcb=(conv_bc_bias, vmem),
        alog_in=(a_log, smem),
        dtb_in=(dt_bias, smem),
        skip_in=(d_skip, smem),
        ggain_in=(gate_gain, vmem),
    )
    HR = R // 2
    outs = dict(out=((M, D), BF16), gtok=((M, D), BF16), small_out=((16, D), F32))
    if ring:
        outs |= dict(g_zx=((HR, 2 * I), F32), g_bc=((HR, 2 * N), F32), g_out=((HR, I), F32))
    else:
        outs |= dict(dw=((D, W), BF16))
    scratch = dict(
        tokens=((M, D), BF16),
        cot=((M, D), BF16),
        w=((D, W), BF16),
        wdt=((LANES, D), BF16),
        xn=((M, D), BF16),
        xnt=((D, M), BF16),
        gt=((D, M), BF16),
        rowm=((B, 9, 8, Q), F32),
        conv=((8, KX), F32),
        rate=((HP, LANES), F32),
        dtb=((HP, LANES), F32),
        skip=((1, I), F32),
        ggain=((1, I), F32),
        gain=((1, D), F32),
        z=((M, I), BF16),
        vext=((B, T + 8, KX), F32),
        dh=((M, I), F32),
        dtr=((HP, M), F32),
        dt=((HP, M), F32),
        cum=((HP, M), F32),
        cols=((M, LANES), F32),
        dt_wide=((M, I), F32),
        gate_wide=((M, I), F32),
        tail_wide=((M, I), F32),
        dsilu=((M, KX), F32),
        xc=((M, I), BF16),
        xdt=((M, I), BF16),
        xt=((M, I), BF16),
        bm=((M, N), BF16),
        cm=((M, N), BF16),
        ct=((M, N), BF16),
        own_state=((B, NC, N, I), F32),
        state=((B, NC + 1, N, I), F32),
        ys=((M, I), F32),
        yg=((M, I), F32),
        norms=((B, 8, T), F32),
        norms_in=((B, tensor - 1, 8, T), F32),
        inners=((B, 8, T), F32),
        inners_in=((B, tensor - 1, 8, T), F32),
        r2=((M, LANES), F32),
        h=((M, I), BF16),
        dcat=((M, KW), BF16),
        dy=((M, I), BF16),
        dyg=((M, I), BF16),
        own_dstate=((B, NC, N, I), F32),
        dstate=((B, NC + 1, N, I), F32),
        po=((B, 2, 2, T // 4, D), BF16),
        po_in1=((B, 2, 2, T // 4, D // 2), BF16),
        po_in2=((B, 2, T // 4, D // 2), BF16),
        po_mid=((B, 2, T // 4, D // 2), BF16),
        dxdt=((M, I), F32),
        dbc=((M, 2 * N), F32),
        duext=((B, T + 8, KX), F32),
        ddtr=((16, M), BF16),
        dxp=((2 * B, 2, 2, T // 8, D), BF16),
        dx_in1=((2 * B, 2, 2, T // 8, D // 2), BF16),
        dx_in2=((2 * B, 2, T // 8, D // 2), BF16),
        dx_mid=((2 * B, 2, T // 8, D // 2), BF16),
        taps=((5, 8, KX), F32),
        sums=((2, 8, I), F32),
        heads=((2, HP, Q), F32),
        small=((16, D), F32),
        norm_own=((1, D), F32),
    )
    if ring:
        scratch |= dict(
            wdt_in=((dp - 1, H, R), BF16),
            dw=((dp, 2, HR, W), BF16),
            dw_pair=((dp, HR, W), BF16),
            dw_chip=((dp, HR, W), BF16),
            dw_in=((dp - 1, HR, W), BF16),
            small_pair=((1, 16, D), F32),
            small_chip=((16, D), F32),
            small_in=((dp - 1, 16, D), F32),
            small_dp=((8, D), F32),
            small_t=((tensor - 1, 8, D), F32),
            norm_t=((tensor - 1, 1, D), F32),
            norm_plane=((1, D), F32),
            norm_pair=((1, 1, D), F32),
            norm_chip=((1, D), F32),
            norm_in=((dp - 1, 1, D), F32),
            bc_own=((HR, 2 * N), F32),
            bc_in=((tensor - 1, HR, 2 * N), F32),
        )
    names = list(ins) + list(outs) + list(scratch) + ["send", "recv", "local"]

    def kernel(*refs):
        body(g, SimpleNamespace(**dict(zip(names, refs))))

    keep = ("out", "gtok", "small_out", "g_zx") if ring else ()
    res = pl.pallas_call(
        kernel,
        out_shape=[(pltpu.VMEM if n in keep else jax.ShapeDtypeStruct)(s, k) for n, (s, k) in outs.items()],
        in_specs=[m for _, m in ins.values()],
        out_specs=[vmem for _ in outs],
        scratch_shapes=[pltpu.VMEM(s, k) for s, k in scratch.values()]
        + [
            pltpu.SemaphoreType.DMA((SENDS,)),
            pltpu.SemaphoreType.DMA((COPIES,)),
            pltpu.SemaphoreType.DMA((4,)),
        ],
        compiler_params=pltpu.CompilerParams(
            collective_id=0, has_side_effects=True, vmem_limit_bytes=VMEM_LIMIT
        ),
        name="layer",
    )(*[a for a, _ in ins.values()])
    rows = D // (dp * context)
    if ring:
        res = [pltpu.with_memory_space_constraint(a, pltpu.VMEM if n in keep else pltpu.HBM) for n, a in zip(outs, res)]
        ends = dict(
            out=((M, D), BF16, anywhere),
            gtok=((M, D), BF16, anywhere),
            g_norm=((D,), F32, vmem),
            g_zx=((rows, 2, I), F32, anywhere),
            g_bc=((rows, 2 * N), F32, anywhere),
            g_dt=((H, rows), F32, vmem),
            g_cx=((4, I), F32, vmem),
            g_cxb=((I,), F32, vmem),
            g_cbc=((4, 2 * N), F32, vmem),
            g_cbcb=((2 * N,), F32, vmem),
            g_alog=((H,), F32, vmem),
            g_dtb=((H,), F32, vmem),
            g_skip=((H,), F32, vmem),
            g_gain=((I,), F32, vmem),
            g_out=((rows, I), F32, anywhere),
        )
        end_names = ["out_v", "gtok_v", "small_v", "zx_v", "bc_v", "wo_v"] + list(ends) + ["sem", "bc", "wo"]

        def last(*refs):
            hand_out(g, SimpleNamespace(**dict(zip(end_names, refs))))

        res = pl.pallas_call(
            last,
            out_shape=[jax.ShapeDtypeStruct(s, k) for s, k, _ in ends.values()],
            in_specs=[vmem if n in keep else pl.BlockSpec(memory_space=pltpu.HBM) for n in outs],
            out_specs=[m for _, _, m in ends.values()],
            scratch_shapes=[
                pltpu.SemaphoreType.DMA((8,)),
                pltpu.VMEM((HR, 2 * N), F32),
                pltpu.VMEM((HR, I), F32),
            ],
            compiler_params=pltpu.CompilerParams(vmem_limit_bytes=4 << 20),
            name="hand_out",
        )(*res)
        res = dict(zip(ends, res))
        res["out"], res["gtok"] = res["out"].reshape(B, T, D), res["gtok"].reshape(B, T, D)
        res["g_dt"] = res["g_dt"].T
        return tuple(res.values())
    res = dict(zip(outs, res))
    small = lax.psum(res["small_out"], ("dp", "context"))
    every = lax.psum(small, "tensor")
    row, col = lax.broadcasted_iota(jnp.int32, small.shape, 0), lax.broadcasted_iota(jnp.int32, small.shape, 1)
    shared = (row == 7) | ((row < 5) & (col >= I) & (col < KX))
    small = jnp.where(shared, every, small)
    dw = lax.psum_scatter(res["dw"].astype(F32), ("dp", "context"), scatter_dimension=0, tiled=True)
    first = (lax.axis_index("dp") * context + lax.axis_index("context")) * rows
    return (
        res["out"].reshape(B, T, D),
        res["gtok"].reshape(B, T, D),
        small[7],
        jnp.stack([dw[:, 0:I], dw[:, KW:]], 1),
        lax.psum(dw[:, 2 * I : KW], "tensor"),
        lax.dynamic_slice(small, (8, first), (H, rows)).T,
        small[0:4, 0:I],
        small[4, 0:I],
        small[0:4, I:KX],
        small[4, I:KX],
        small[0:H, KX],
        small[0:H, KX + 1],
        small[6, 0:I].reshape(H, I // H).sum(-1),
        small[5, 0:I],
        dw[:, I : 2 * I],
    )


def solution(mesh):
    placed = (
        P("dp", "context", None),
        P("dp", None),
        P("dp", "context", None),
        P(),
        P("dp", None, "tensor"),
        P("dp", None),
        P("dp", "tensor"),
        P(None, "tensor"),
        P("tensor"),
        P(),
        P(),
        P("tensor"),
        P("tensor"),
        P("tensor"),
        P("tensor"),
        P("dp", "tensor"),
    )
    sizes = tuple(mesh.shape[a] for a in ("dp", "context", "tensor"))
    return jax.shard_map(
        functools.partial(per_device, sizes),
        mesh=mesh,
        in_specs=placed,
        out_specs=(
            P("dp", "context", None),
            P("dp", "context", None),
            P(),
            P(("dp", "context"), None, "tensor"),
            P(("dp", "context"), None),
            P(("dp", "context"), "tensor"),
            P(None, "tensor"),
            P("tensor"),
            P(),
            P(),
            P("tensor"),
            P("tensor"),
            P("tensor"),
            P("tensor"),
            P(("dp", "context"), "tensor"),
        ),
        check_vma=False,
    )
```
